256 devices in a mesh: graph: 32 (over z, x_hi, core), feat: 8 (over x_lo, y).
Axes of the slice: x: 4 (x_hi: 2, x_lo: 2; x = x_hi * 2 + x_lo), y: 4, z: 8, core: 2. Of those that a mesh axis runs over, the one named last changes fastest.
Arguments:
- features: bfloat16 [256, 65536], P('feat', 'graph'), may hold values from -6 to 6
- tiles: bfloat16 [8192, 128, 128], P('graph'), may hold values from 0 to 0.049316406
- tile_source: int32 [8192], P('graph'), may hold values from 0 to 511, as said below
- tile_target: int32 [8192], P('graph'), may hold values from 0 to 15
- tile_count: int32 [32], P('graph'), may hold values from 88 to 256, as said below
- weight: bfloat16 [256, 256], replicated, may hold values from -0.375 to 0.375
Outputs:
- layer_output: bfloat16 [256, 65536], P('feat', 'graph')
The draws below stay inside these ranges and needn't reach their ends.
Inputs may be any that keep to these rules, and one draw needn't show every extreme that they name: Within the 256 slots of each slab, the source slab tile_source // 16 never falls from one slot to the next. The used slots of a slab hold at least one tile from every slab's node blocks and at most 16 from any one slab's, and exactly 16 from some slab's, on every slab. `tile_count`: some slab uses all 256 slots.
All inputs are finite; a program needn't handle non-finite values.
Results may differ from the reference program's by a relative error of at most 0.0049.
Values may be sent and summed in bfloat16 or wider, within the bound.
No kernel may reach another device: no remote copies, remote signals or barrier semaphores. Data moves between devices by JAX's collectives and lax.ppermute only.
A program may use at most 64 MiB of HBM per device.

```python
import jax
import jax.numpy as jnp
from jax import lax

H = 256
BLK = 128
SLAB_BLOCKS = 16
PAIR_MOST = 16
TILES_DEV = 256
NODE_BLOCKS = 512
NODES = 65536
TILES = 8192
N_GRAPH = 32


def tile_plan(key):
    slab_count = N_GRAPH
    extra_most = TILES_DEV - slab_count
    indices = jnp.arange(slab_count)
    extra_loads = jax.random.randint(jax.random.fold_in(key, 11), (slab_count,), extra_most // 4, extra_most + 1)
    heaviest = jax.random.randint(jax.random.fold_in(key, 12), (), 0, slab_count)
    extra_loads = jnp.where(indices == heaviest, extra_most, extra_loads)
    distance = jnp.abs(indices[None, :] - indices[:, None])
    distance = jnp.minimum(distance, slab_count - distance)
    jitter = jax.random.randint(jax.random.fold_in(key, 13), (slab_count, slab_count), 0, slab_count)
    scores = (2 * distance + jitter) * slab_count + indices[None, :]
    pair_ranks = jnp.argsort(jnp.argsort(scores, axis=1), axis=1)
    counts = 1 + jnp.clip(extra_loads[:, None] - (PAIR_MOST - 1) * pair_ranks, 0, PAIR_MOST - 1)
    slot_ends = jnp.cumsum(counts, axis=1)
    slot_numbers = jnp.arange(TILES_DEV)
    slab_of_slot = jnp.sum((slot_ends[:, None, :] <= slot_numbers[None, :, None]).astype(jnp.int32), axis=2)
    slab_of_slot = jnp.minimum(slab_of_slot, slab_count - 1)
    source_blocks = jax.random.randint(jax.random.fold_in(key, 14), (slab_count, TILES_DEV), 0, SLAB_BLOCKS)
    target_blocks = jax.random.randint(jax.random.fold_in(key, 15), (slab_count, TILES_DEV), 0, SLAB_BLOCKS)
    source_ids = (slab_of_slot * SLAB_BLOCKS + source_blocks).reshape(-1).astype(jnp.int32)
    target_ids = target_blocks.reshape(-1).astype(jnp.int32)
    used_counts = slot_ends[:, -1].astype(jnp.int32)
    return (source_ids, target_ids, used_counts)


def draw_tile_source(key, part):
    return tile_plan(key)[0]


def draw_tile_target(key, part):
    return tile_plan(key)[1]


def draw_tile_count(key, part):
    return tile_plan(key)[2]


def shard_levels(rng, shape, cuts, low, largest):
    gain = 1.0
    for axis_at, parts in cuts:
        draws = jax.random.uniform(jax.random.fold_in(jax.random.fold_in(rng, 6), axis_at), (parts,), jnp.float32, low / len(cuts), largest / len(cuts))
        gain = gain * jnp.repeat(jnp.exp(draws), shape[axis_at] // parts).reshape((-1,) + (1,) * (len(shape) - 1 - axis_at))
    return gain


def gaussian(own_key, extent, width, bound, cuts=(), held_as=jnp.bfloat16):
    drawn = jax.random.normal(own_key, extent, jnp.float32) * width
    if len(cuts) > 0:
        drawn = shard_levels(own_key, extent, cuts, -0.22, 0.18) * drawn
    return jnp.clip(drawn, min=-bound, max=bound).astype(held_as)


def setup_inputs(seed: int = 0) -> dict:
    arg_keys = jax.random.split(jax.random.key(seed), 7)
    return {
        "features": gaussian(arg_keys[0], (H, NODES), 1.0, 6.0, ((0, 8), (1, 32))),
        "tiles": jnp.clip(0.049316406 * jax.random.uniform(arg_keys[1], (TILES, BLK, BLK), jnp.float32) ** shard_levels(arg_keys[1], (TILES, BLK, BLK), ((0, 32),), -0.2, 0.2), 0.0, 0.049316406).astype(jnp.bfloat16),
        "tile_source": draw_tile_source(jax.random.fold_in(arg_keys[6], 71), 0),
        "tile_target": draw_tile_target(jax.random.fold_in(arg_keys[6], 71), 0),
        "tile_count": draw_tile_count(jax.random.fold_in(arg_keys[6], 71), 0),
        "weight": gaussian(arg_keys[5], (H, H), H ** -0.5, 0.375),
    }


def slab_aggregate(feature_blocks, tile_group, source_group, target_group, count_value):
    usable = jnp.arange(TILES_DEV) < count_value
    picked = jnp.take(feature_blocks, source_group, axis=1).astype(jnp.float32)
    products = jnp.einsum('hwj,wij->hwi', picked, tile_group.astype(jnp.float32), precision=lax.Precision.HIGHEST)
    select = ((target_group[:, None] == jnp.arange(SLAB_BLOCKS)[None, :]) & usable[:, None]).astype(jnp.float32)
    return jnp.einsum('hwi,wb->hbi', products, select, precision=lax.Precision.HIGHEST)


def reference(features, tiles, tile_source, tile_target, tile_count, weight):
    blocks = features.reshape(H, NODE_BLOCKS, BLK)
    grouped = (tiles.reshape(N_GRAPH, TILES_DEV, BLK, BLK), tile_source.reshape(N_GRAPH, TILES_DEV), tile_target.reshape(N_GRAPH, TILES_DEV), tile_count)
    per_slab = lax.map(lambda members: slab_aggregate(blocks, members[0], members[1], members[2], members[3]), grouped)
    aggregate = jnp.transpose(per_slab, (1, 0, 2, 3)).reshape(H, NODES)
    rounded = aggregate.astype(jnp.bfloat16)
    summed = jnp.dot(weight.T, rounded, preferred_element_type=jnp.float32)
    return jnp.maximum(summed, 0.0).astype(jnp.bfloat16)
```

```python
import functools

import jax
import jax.numpy as jnp
from jax import lax
from jax.experimental import pallas as pl
from jax.experimental.pallas import tpu as pltpu
from jax.sharding import PartitionSpec as P

PAIR_MOST = 16
GROUP = 8
DEPTH = 8


def place(z, half, core):
    return (z % DEPTH) * 4 + half * 2 + core


def route(block, move):
    pairs = []
    for z in range(DEPTH):
        for half in range(2):
            for core in range(2):
                pairs.append((place(z, half, core), place(*move(z, half, core))))
    return lax.ppermute(block, "graph", pairs)


def swap_core(block):
    return route(block, lambda z, half, core: (z, half, 1 - core))


def swap_half(block):
    return route(block, lambda z, half, core: (z, 1 - half, core))


def along_z(block):
    return route(block, lambda z, half, core: (z + 1 - 2 * core, half, core))


def tile_kernel(layout, first_piece, begins, ends, *refs):
    piece_count = sum(layout)
    refs = list(refs)
    meta = refs.pop(0)
    total_in = None if begins else refs.pop(0)
    visitors = [refs.pop(0) for _ in layout]
    tiles = refs.pop(0)
    out = refs.pop(0)
    window, arrived = refs[0], refs[1]
    total = refs[2] if ends else out
    side = tiles.shape[1]
    slot_total = tiles.shape[0] // side
    rows = visitors[0].shape[-2]
    block_count = visitors[0].shape[-1] // side

    bounds = []
    copies = []
    for piece in range(piece_count):
        start = meta[2 * slot_total + first_piece + piece]
        end = meta[2 * slot_total + 32 + first_piece + piece]
        low = jnp.minimum(start, slot_total - PAIR_MOST)
        copy = pltpu.make_async_copy(
            tiles.at[pl.ds(pl.multiple_of(low * side, side), PAIR_MOST * side), :],
            window.at[piece],
            arrived.at[piece],
        )
        copy.start()
        bounds.append((start, end, low))
        copies.append(copy)
    if begins:
        total[...] = jnp.zeros_like(total)
    elif ends:
        total[...] = total_in[...]

    piece = 0
    for visitor, parts in zip(visitors, layout):
        for part in range(parts):
            start, end, low = bounds[piece]
            copies[piece].wait()

            def group(turn, carry, visitor=visitor, part=part, piece=piece, start=start, end=end, low=low):
                wanted = start + turn * GROUP
                base = jnp.minimum(wanted, low + PAIR_MOST - GROUP)
                products = []
                for unit in range(0, GROUP, 2):
                    sources = []
                    for other in range(2):
                        lane = pl.multiple_of(meta[base + unit + other] * side, side)
                        sources.append(visitor[part, :, pl.ds(lane, side)])
                    pair = window[
                        piece, pl.ds(pl.multiple_of((base - low + unit) * side, side), 2 * side), :
                    ]
                    both = lax.dot_general(
                        jnp.concatenate(sources, 0),
                        pair,
                        (((1,), (1,)), ((), ())),
                        preferred_element_type=jnp.float32,
                    )
                    products += [both[:rows, :side], both[rows:, side:]]
                for unit in range(GROUP):
                    slot = base + unit
                    fits = (slot >= wanted) & (slot < end)
                    target = jnp.where(fits, meta[slot_total + slot], block_count)
                    at = pl.ds(pl.multiple_of(target * rows, rows), rows)
                    total[at, :] += products[unit]
                return carry

            lax.fori_loop(0, (end - start + GROUP - 1) // GROUP, group, 0)
            piece += 1
    if ends:
        copies_out = out.shape[0] // rows
        for block in range(block_count):
            value = total[block * rows : (block + 1) * rows, :].astype(jnp.bfloat16)
            for copy in range(copies_out):
                out[copy * rows : (copy + 1) * rows, block * side : (block + 1) * side] = value


def add_tiles(meta, total, visitors, tiles, first_piece, ends=False):
    layout = tuple(visitor.shape[0] for visitor in visitors)
    begins = total is None
    side = tiles.shape[1]
    rows, nodes = visitors[0].shape[-2:]
    total_rows = (nodes // side + 1) * rows
    pieces = sum(layout)
    vmem = pl.BlockSpec(memory_space=pltpu.VMEM)
    in_specs = [pl.BlockSpec(memory_space=pltpu.SMEM)]
    args = [meta]
    aliases = {}
    if not begins:
        in_specs.append(vmem)
        args.append(total)
        if not ends:
            aliases = {1: 0}
    in_specs += [vmem] * len(visitors) + [pl.BlockSpec(memory_space=pl.ANY)]
    args += list(visitors) + [tiles]
    out_shape = jax.ShapeDtypeStruct((total_rows, side), jnp.float32)
    scratch = [
        pltpu.VMEM((pieces, PAIR_MOST * side, side), jnp.bfloat16),
        pltpu.SemaphoreType.DMA((pieces,)),
    ]
    if ends:
        out_shape = jax.ShapeDtypeStruct((8 * rows, nodes), jnp.bfloat16)
        scratch.append(pltpu.VMEM((total_rows, side), jnp.float32))
    return pl.pallas_call(
        functools.partial(tile_kernel, layout, first_piece, begins, ends),
        out_shape=out_shape,
        in_specs=in_specs,
        out_specs=vmem,
        scratch_shapes=scratch,
        input_output_aliases=aliases,
        compiler_params=pltpu.CompilerParams(vmem_limit_bytes=16 << 20),
        cost_estimate=pl.CostEstimate(
            flops=pieces * 2 * PAIR_MOST * rows * side * side,
            bytes_accessed=pieces * PAIR_MOST * side * side * 2,
            transcendentals=0,
        ),
    )(*args)


def slabs_in_order(position):
    z, half, core = position // 4, (position // 2) % 2, position % 2

    def at(step, far, other):
        return ((z + step) % DEPTH) * 4 + (half + far) % 2 * 2 + (core + other) % 2

    mine = 2 * core - 1
    order = [at(0, far, other) for far in range(2) for other in range(2)]
    for turn in range(1, 4):
        for far in range(2):
            order += [at(mine * turn, far, 0), at(mine * turn, far, 1)]
            order += [at(-mine * turn, far, 1), at(-mine * turn, far, 0)]
    order += [at(4, far, other) for far in range(2) for other in range(2)]
    return jnp.stack(order)


def body(features, tiles, tile_source, tile_target, tile_count, weight):
    feature_rows, slab_nodes = features.shape
    slot_total, side, _ = tiles.shape
    block_count = slab_nodes // side
    flat_tiles = tiles.reshape(slot_total * side, side)

    own = features[None]
    sibling = swap_core(own)
    far = swap_half(own)
    near_pair = jnp.concatenate([own, sibling], 0)
    far_sibling = swap_core(far)
    far_pair = jnp.concatenate([far, far_sibling], 0)

    order = slabs_in_order(lax.axis_index("graph"))
    usable = jnp.arange(slot_total) < tile_count[0]
    slab = jnp.where(usable, tile_source // block_count, 2 * slab_nodes)
    starts = jnp.sum((slab[None, :] < order[:, None]).astype(jnp.int32), 1)
    stops = jnp.sum((slab[None, :] <= order[:, None]).astype(jnp.int32), 1)
    meta = jnp.concatenate([tile_source % block_count, tile_target, starts, stops])

    total = add_tiles(meta, None, [near_pair, far_pair], flat_tiles, 0)
    near, away = near_pair, far_pair
    for turn in range(1, 4):
        near = along_z(near)
        away = along_z(away)
        near_other = swap_core(near)
        away_other = swap_core(away)
        total = add_tiles(meta, total, [near, near_other], flat_tiles, 8 * turn - 4)
        total = add_tiles(meta, total, [away, away_other], flat_tiles, 8 * turn)
    near = along_z(near[:1])
    away = along_z(away[:1])
    repeated = add_tiles(
        meta, total, [near, swap_core(near), away, swap_core(away)], flat_tiles, 28, True
    )
    everyone = lax.all_to_all(repeated, "feat", 0, 0, tiled=True)
    columns = lax.dynamic_slice_in_dim(
        weight, lax.axis_index("feat") * feature_rows, feature_rows, 1
    )
    combined = jnp.einsum(
        "ko,kn->on", columns, everyone, preferred_element_type=jnp.float32
    )
    return jnp.maximum(combined, 0.0).astype(jnp.bfloat16)


def solution(mesh):
    return jax.shard_map(
        body,
        mesh=mesh,
        in_specs=(
            P("feat", "graph"),
            P("graph", None, None),
            P("graph"),
            P("graph"),
            P("graph"),
            P(),
        ),
        out_specs=P("feat", "graph"),
        check_vma=False,
    )
```

```python
import functools

import jax
import jax.numpy as jnp
from jax import lax
from jax.experimental import pallas as pl
from jax.experimental.pallas import tpu as pltpu
from jax.sharding import PartitionSpec as P

PAIR_MOST = 16
GROUP = 8
DEPTH = 8


def place(z, half, core):
    return (z % DEPTH) * 4 + half * 2 + core


def route(block, move):
    pairs = []
    for z in range(DEPTH):
        for half in range(2):
            for core in range(2):
                pairs.append((place(z, half, core), place(*move(z, half, core))))
    return lax.ppermute(block, "graph", pairs)


def swap_core(block):
    return route(block, lambda z, half, core: (z, half, 1 - core))


def swap_half(block):
    return route(block, lambda z, half, core: (z, 1 - half, core))


def along_z(block):
    return route(block, lambda z, half, core: (z + 1 - 2 * core, half, core))


def tile_kernel(layout, first_piece, begins, ends, *refs):
    piece_count = sum(layout)
    refs = list(refs)
    meta = refs.pop(0)
    total_in = None if begins else refs.pop(0)
    visitors = [refs.pop(0) for _ in layout]
    tiles = refs.pop(0)
    out = refs.pop(0)
    window, arrived = refs[0], refs[1]
    total = refs[2] if ends else out
    side = tiles.shape[1]
    slot_total = tiles.shape[0] // side
    rows = visitors[0].shape[-2]
    block_count = visitors[0].shape[-1] // side

    bounds = []
    copies = []
    for piece in range(piece_count):
        start = meta[2 * slot_total + first_piece + piece]
        end = meta[2 * slot_total + 32 + first_piece + piece]
        low = jnp.minimum(start, slot_total - PAIR_MOST)
        copy = pltpu.make_async_copy(
            tiles.at[pl.ds(pl.multiple_of(low * side, side), PAIR_MOST * side), :],
            window.at[piece],
            arrived.at[piece],
        )
        copy.start()
        bounds.append((start, end, low))
        copies.append(copy)
    if begins:
        total[...] = jnp.zeros_like(total)
    elif ends:
        total[...] = total_in[...]

    piece = 0
    for visitor, parts in zip(visitors, layout):
        for part in range(parts):
            start, end, low = bounds[piece]
            copies[piece].wait()

            def group(turn, carry, visitor=visitor, part=part, piece=piece, start=start, end=end, low=low):
                wanted = start + turn * GROUP
                base = jnp.minimum(wanted, low + PAIR_MOST - GROUP)
                products = []
                for unit in range(0, GROUP, 2):
                    sources = []
                    for other in range(2):
                        lane = pl.multiple_of(meta[base + unit + other] * side, side)
                        sources.append(visitor[part, :, pl.ds(lane, side)])
                    pair = window[
                        piece, pl.ds(pl.multiple_of((base - low + unit) * side, side), 2 * side), :
                    ]
                    both = lax.dot_general(
                        jnp.concatenate(sources, 0),
                        pair,
                        (((1,), (1,)), ((), ())),
                        preferred_element_type=jnp.float32,
                    )
                    products += [both[:rows, :side], both[rows:, side:]]
                for unit in range(GROUP):
                    slot = base + unit
                    fits = (slot >= wanted) & (slot < end)
                    target = jnp.where(fits, meta[slot_total + slot], block_count)
                    at = pl.ds(pl.multiple_of(target * rows, rows), rows)
                    total[at, :] += products[unit]
                return carry

            lax.fori_loop(0, (end - start + GROUP - 1) // GROUP, group, 0)
            piece += 1
    if ends:
        copies_out = out.shape[0] // rows
        for block in range(block_count):
            value = total[block * rows : (block + 1) * rows, :].astype(jnp.bfloat16)
            for copy in range(copies_out):
                out[copy * rows : (copy + 1) * rows, block * side : (block + 1) * side] = value


def add_tiles(meta, total, visitors, tiles, first_piece, ends=False):
    layout = tuple(visitor.shape[0] for visitor in visitors)
    begins = total is None
    side = tiles.shape[1]
    rows, nodes = visitors[0].shape[-2:]
    total_rows = (nodes // side + 1) * rows
    pieces = sum(layout)
    vmem = pl.BlockSpec(memory_space=pltpu.VMEM)
    in_specs = [pl.BlockSpec(memory_space=pltpu.SMEM)]
    args = [meta]
    aliases = {}
    if not begins:
        in_specs.append(vmem)
        args.append(total)
        if not ends:
            aliases = {1: 0}
    in_specs += [vmem] * len(visitors) + [pl.BlockSpec(memory_space=pltpu.HBM)]
    args += list(visitors) + [tiles]
    out_shape = jax.ShapeDtypeStruct((total_rows, side), jnp.float32)
    scratch = [
        pltpu.VMEM((pieces, PAIR_MOST * side, side), jnp.bfloat16),
        pltpu.SemaphoreType.DMA((pieces,)),
    ]
    if ends:
        out_shape = jax.ShapeDtypeStruct((8 * rows, nodes), jnp.bfloat16)
        scratch.append(pltpu.VMEM((total_rows, side), jnp.float32))
    return pl.pallas_call(
        functools.partial(tile_kernel, layout, first_piece, begins, ends),
        out_shape=out_shape,
        in_specs=in_specs,
        out_specs=vmem,
        scratch_shapes=scratch,
        input_output_aliases=aliases,
        compiler_params=pltpu.CompilerParams(vmem_limit_bytes=16 << 20),
        cost_estimate=pl.CostEstimate(
            flops=pieces * 2 * PAIR_MOST * rows * side * side,
            bytes_accessed=pieces * PAIR_MOST * side * side * 2,
            transcendentals=0,
        ),
    )(*args)


def slabs_in_order(position):
    z, half, core = position // 4, (position // 2) % 2, position % 2

    def at(step, far, other):
        return ((z + step) % DEPTH) * 4 + (half + far) % 2 * 2 + (core + other) % 2

    mine = 2 * core - 1
    order = [at(0, far, other) for far in range(2) for other in range(2)]
    for turn in range(1, 4):
        for far in range(2):
            order += [at(mine * turn, far, 0), at(mine * turn, far, 1)]
            order += [at(-mine * turn, far, 1), at(-mine * turn, far, 0)]
    order += [at(4, far, other) for far in range(2) for other in range(2)]
    return jnp.stack(order)


def body(features, tiles, tile_source, tile_target, tile_count, weight):
    feature_rows, slab_nodes = features.shape
    slot_total, side, _ = tiles.shape
    block_count = slab_nodes // side
    flat_tiles = tiles.reshape(slot_total * side, side)

    own = features[None]
    sibling = swap_core(own)
    far = swap_half(own)
    near_pair = jnp.concatenate([own, sibling], 0)
    far_sibling = swap_core(far)
    far_pair = jnp.concatenate([far, far_sibling], 0)

    order = slabs_in_order(lax.axis_index("graph"))
    usable = jnp.arange(slot_total) < tile_count[0]
    slab = jnp.where(usable, tile_source // block_count, 2 * slab_nodes)
    starts = jnp.sum((slab[None, :] < order[:, None]).astype(jnp.int32), 1)
    stops = jnp.sum((slab[None, :] <= order[:, None]).astype(jnp.int32), 1)
    meta = jnp.concatenate([tile_source % block_count, tile_target, starts, stops])

    total = add_tiles(meta, None, [near_pair, far_pair], flat_tiles, 0)
    near, away = near_pair, far_pair
    for turn in range(1, 4):
        near = along_z(near)
        away = along_z(away)
        near_other = swap_core(near)
        away_other = swap_core(away)
        total = add_tiles(meta, total, [near, near_other], flat_tiles, 8 * turn - 4)
        total = add_tiles(meta, total, [away, away_other], flat_tiles, 8 * turn)
    near = along_z(near)
    away = along_z(away)
    total = add_tiles(meta, total, [near], flat_tiles, 28)
    repeated = add_tiles(meta, total, [away], flat_tiles, 30, True)
    everyone = lax.all_to_all(repeated, "feat", 0, 0, tiled=True)
    columns = lax.dynamic_slice_in_dim(
        weight, lax.axis_index("feat") * feature_rows, feature_rows, 1
    )
    combined = jnp.einsum(
        "ko,kn->on", columns, everyone, preferred_element_type=jnp.float32
    )
    return jnp.maximum(combined, 0.0).astype(jnp.bfloat16)


def solution(mesh):
    return jax.shard_map(
        body,
        mesh=mesh,
        in_specs=(
            P("feat", "graph"),
            P("graph", None, None),
            P("graph"),
            P("graph"),
            P("graph"),
            P(),
        ),
        out_specs=P("feat", "graph"),
        check_vma=False,
    )
```

```python
import functools

import jax
import jax.numpy as jnp
from jax import lax
from jax.experimental import pallas as pl
from jax.experimental.pallas import tpu as pltpu
from jax.sharding import PartitionSpec as P

PAIR_MOST = 16
GROUP = 16
DEPTH = 8


def place(z, half, core):
    return (z % DEPTH) * 4 + half * 2 + core


def route(block, move):
    pairs = []
    for z in range(DEPTH):
        for half in range(2):
            for core in range(2):
                pairs.append((place(z, half, core), place(*move(z, half, core))))
    return lax.ppermute(block, "graph", pairs)


def swap_core(block):
    return route(block, lambda z, half, core: (z, half, 1 - core))


def swap_half(block):
    return route(block, lambda z, half, core: (z, 1 - half, core))


def along_z(block):
    return route(block, lambda z, half, core: (z + 1 - 2 * core, half, core))


def tile_kernel(flips, first_pair, begins, ends, *refs):
    refs = list(refs)
    meta = refs.pop(0)
    total_in = None if begins else refs.pop(0)
    visitors = [refs.pop(0) for _ in flips]
    tiles = refs.pop(0)
    out = refs.pop(0)
    total = refs[0] if ends else out
    side = tiles.shape[1]
    slot_total = tiles.shape[0] // side
    rows = visitors[0].shape[-2]
    block_count = visitors[0].shape[-1] // side

    bounds = []
    for pair in range(len(flips)):
        start = meta[2 * slot_total + first_pair + pair]
        end = meta[2 * slot_total + 16 + first_pair + pair]
        bounds.append((start, end, (end - start + GROUP - 1) // GROUP))

    if begins:
        total[...] = jnp.zeros_like(total)
    elif ends:
        total[...] = total_in[...]

    for pair, (start, end, turns) in enumerate(bounds):

        def group(turn, carry, pair=pair, start=start, end=end):
            visitor = visitors[pair]
            low = jnp.minimum(start + turn * GROUP, slot_total - GROUP)
            products = []
            for unit in range(GROUP):
                code = meta[low + unit]
                part = code // block_count
                if flips[pair]:
                    part = 1 - part
                lane = pl.multiple_of(code % block_count * side, side)
                products.append(
                    lax.dot_general(
                        visitor[part, :, pl.ds(lane, side)],
                        tiles[pl.ds(pl.multiple_of((low + unit) * side, side), side), :],
                        (((1,), (1,)), ((), ())),
                        preferred_element_type=jnp.float32,
                    )
                )
            for unit in range(GROUP):
                slot = low + unit
                fits = (slot >= start + turn * GROUP) & (slot < end)
                target = jnp.where(fits, meta[slot_total + slot], block_count)
                at = pl.ds(pl.multiple_of(target * rows, rows), rows)
                total[at, :] += products[unit]
            return carry

        lax.fori_loop(0, turns, group, 0)
    if ends:
        shares = out.shape[0]
        nodes = block_count * side
        for block in range(block_count):
            value = total[block * rows : (block + 1) * rows, :].astype(jnp.bfloat16)
            share, lane = divmod(block * side, nodes // shares)
            out[share, :, lane : lane + side] = value


def add_tiles(meta, total, visitors, flips, tiles, first_pair, ends=False):
    begins = total is None
    side = tiles.shape[1]
    rows, nodes = visitors[0].shape[-2:]
    total_rows = (nodes // side + 1) * rows
    pairs = len(visitors)
    vmem = pl.BlockSpec(memory_space=pltpu.VMEM)
    in_specs = [pl.BlockSpec(memory_space=pltpu.SMEM)]
    args = [meta]
    aliases = {}
    if not begins:
        in_specs.append(vmem)
        args.append(total)
        if not ends:
            aliases = {1: 0}
    in_specs += [vmem] * (pairs + 1)
    args += list(visitors) + [tiles]
    out_shape = jax.ShapeDtypeStruct((total_rows, side), jnp.float32)
    scratch = []
    if ends:
        out_shape = jax.ShapeDtypeStruct((8, rows, nodes // 8), jnp.bfloat16)
        scratch.append(pltpu.VMEM((total_rows, side), jnp.float32))
    return pl.pallas_call(
        functools.partial(tile_kernel, flips, first_pair, begins, ends),
        out_shape=out_shape,
        in_specs=in_specs,
        out_specs=vmem,
        scratch_shapes=scratch,
        input_output_aliases=aliases,
        compiler_params=pltpu.CompilerParams(vmem_limit_bytes=16 << 20),
        cost_estimate=pl.CostEstimate(
            flops=pairs * 4 * PAIR_MOST * rows * side * side,
            bytes_accessed=pairs * 2 * PAIR_MOST * side * side * 2,
            transcendentals=0,
        ),
    )(*args)


def pairs_in_order(position):
    z, half, core = position // 4, (position // 2) % 2, position % 2

    def at(step, far):
        return ((z + step) % DEPTH) * 2 + (half + far) % 2

    mine = 2 * core - 1
    order = [at(0, 0), at(0, 1)]
    for turn in range(1, 4):
        for far in range(2):
            order += [at(mine * turn, far), at(-mine * turn, far)]
    order += [at(4, 0), at(4, 1)]
    return jnp.stack(order)


def body(features, tiles, tile_source, tile_target, tile_count, weight):
    feature_rows, slab_nodes = features.shape
    slot_total, side, _ = tiles.shape
    block_count = slab_nodes // side
    flat_tiles = tiles.reshape(slot_total * side, side)

    own = features[None]
    sibling = swap_core(own)
    far = swap_half(own)
    near_pair = jnp.concatenate([own, sibling], 0)
    far_sibling = swap_core(far)
    far_pair = jnp.concatenate([far, far_sibling], 0)

    position = lax.axis_index("graph")
    order = pairs_in_order(position)
    usable = jnp.arange(slot_total) < tile_count[0]
    slab = tile_source // block_count
    pair = jnp.where(usable, slab // 2, 2 * slab_nodes)
    starts = jnp.sum((pair[None, :] < order[:, None]).astype(jnp.int32), 1)
    stops = jnp.sum((pair[None, :] <= order[:, None]).astype(jnp.int32), 1)
    part = (slab + position) % 2
    codes = part * block_count + tile_source % block_count
    meta = jnp.concatenate([codes, tile_target, starts, stops])

    total = add_tiles(meta, None, [near_pair], (0,), flat_tiles, 0)
    total = add_tiles(meta, total, [far_pair], (0,), flat_tiles, 1)
    near, away = near_pair, far_pair
    for turn in range(1, 4):
        near = along_z(near)
        away = along_z(away)
        near_other = swap_core(near)
        away_other = swap_core(away)
        total = add_tiles(meta, total, [near, near_other], (0, 1), flat_tiles, 4 * turn - 2)
        total = add_tiles(meta, total, [away, away_other], (0, 1), flat_tiles, 4 * turn)
    near = along_z(near)
    away = along_z(away)
    total = add_tiles(meta, total, [near], (0,), flat_tiles, 14)
    shared = add_tiles(meta, total, [away], (0,), flat_tiles, 15, True)
    shares, _, share_nodes = shared.shape
    everyone = lax.all_to_all(shared, "feat", 0, 0, tiled=True)
    combined = jnp.einsum(
        "ko,kn->on",
        weight,
        everyone.reshape(shares * feature_rows, share_nodes),
        preferred_element_type=jnp.float32,
    )
    outputs = jnp.maximum(combined, 0.0).astype(jnp.bfloat16)
    mine = lax.all_to_all(
        outputs.reshape(shares, feature_rows, share_nodes), "feat", 0, 0, tiled=True
    )
    return jnp.transpose(mine, (1, 0, 2)).reshape(feature_rows, slab_nodes)


def solution(mesh):
    return jax.shard_map(
        body,
        mesh=mesh,
        in_specs=(
            P("feat", "graph"),
            P("graph", None, None),
            P("graph"),
            P("graph"),
            P("graph"),
            P(),
        ),
        out_specs=P("feat", "graph"),
        check_vma=False,
    )
```
